32 devices in a mesh: alpha: 8 (over z, x), beta: 4 (over y, core).
Axes of the slice: x: 2, y: 2, z: 4, core: 2. Of those that a mesh axis runs over, the one named last changes fastest.
Arguments:
- coeffs: bfloat16 [16384, 16384], P('alpha', 'beta'), may hold values from -6 to 6
- local_coupling: bfloat16 [2, 64, 256, 256], P(None, 'alpha'), may hold values from -0.25 to 0.25
- remote_coupling: bfloat16 [2, 64, 1, 256, 256], P(None, 'alpha'), may hold values from -0.25 to 0.25
- beta_coupling: bfloat16 [2, 16, 1024, 1024], P(None, 'beta'), may hold values from -0.125 to 0.125
- exc_rows: int32 [64, 1, 256], P('alpha'), may hold values from 0 to 16383, as said below
Outputs:
- sigma: bfloat16 [16384, 16384], P('alpha', 'beta')
The draws below stay inside these ranges and needn't reach their ends.
Inputs may be any that keep to these rules, and one draw needn't show every extreme that they name: `exc_rows`: each entry names a global alpha string. Of the 2048 entries that belong to the blocks of one alpha index, at most 512 lie in the rows of any one alpha index; in every draw some alpha index holds exactly 512 of the entries of every alpha index.
All inputs are finite; a program needn't handle non-finite values.
Results may differ from the reference program's by a relative error of at most 0.0059.
Values may be sent and summed in bfloat16 or wider, within the bound.
A program may use at most 320 MiB of HBM per device.

```python
import jax
import jax.numpy as jnp
from jax import lax

N = 16384
ABLK = 256
BORD = 1024
CHANNELS = 2
SLOTS = 1
OWNERS = 8
ROWS = 2048
CAP = 512


def draw_exc_rows(key, part):
    subkeys = jax.random.split(key, 3)
    favor = jax.random.randint(subkeys[0], (OWNERS,), 0, 1 << 14)
    favored = jax.random.randint(subkeys[1], (), 0, OWNERS)
    favor = jnp.where(jnp.arange(OWNERS) == favored, 1 << 16, favor)

    def one_device(device_id):
        device_key = jax.random.fold_in(subkeys[2], device_id)
        pieces = jax.random.split(device_key, 3)
        jitter = jax.random.randint(pieces[0], (OWNERS, CAP), 0, 1 << 13)
        scores = (jitter + favor[:, None]).reshape(-1)
        ranked = jnp.argsort(-scores, stable=True)
        chosen = ranked[:ROWS * SLOTS]
        owner_of = (chosen // CAP).astype(jnp.int32)
        shuffled = jax.random.permutation(pieces[1], owner_of)
        offset = jax.random.randint(pieces[2], (ROWS * SLOTS,), 0, ROWS)
        return (shuffled * ROWS + offset).astype(jnp.int32)
    requests = jax.vmap(one_device)(jnp.arange(OWNERS, dtype=jnp.int32))
    requests = requests.reshape(OWNERS, ROWS // ABLK, SLOTS, ABLK)
    return requests.reshape(N // ABLK, SLOTS, ABLK)


def block_levels(stream_key, shape, cuts, smallest, top_value):
    gain, own = 1.0, jax.random.fold_in(stream_key, 6)
    for axis_at, parts in cuts:
        heights = jnp.exp(jax.random.uniform(jax.random.fold_in(own, axis_at), (parts,), jnp.float32, smallest / len(cuts), top_value / len(cuts)))
        gain = gain * jnp.repeat(heights, shape[axis_at] // parts).reshape([-1 if axis == axis_at else 1 for axis in range(len(shape))])
    return gain


def normal_values(key, dims, scale, limit, cuts=(), kind=jnp.bfloat16):
    drawn = scale * jax.random.normal(key, dims, jnp.float32)
    if cuts:
        drawn = drawn * block_levels(key, dims, cuts, -0.22, 0.18)
    return jnp.clip(drawn, -limit, limit).astype(kind)


def setup_inputs(seed: int = 0) -> dict:
    seeds = jax.random.split(jax.random.key(seed), 6)
    coeffs = normal_values(seeds[0], (N, N), 1.0, 6.0, ((0, 8), (1, 4)))
    local_coupling = normal_values(seeds[1], (CHANNELS, N // ABLK, ABLK, ABLK), (ABLK * (SLOTS + 1)) ** -0.5, 0.25, ((1, 8),))
    remote_coupling = normal_values(seeds[2], (CHANNELS, N // ABLK, SLOTS, ABLK, ABLK), (ABLK * (SLOTS + 1)) ** -0.5, 0.25, ((1, 8),))
    beta_coupling = normal_values(seeds[3], (CHANNELS, N // BORD, BORD, BORD), (BORD * CHANNELS) ** -0.5, 0.125, ((1, 4),))
    exc_rows = draw_exc_rows(jax.random.fold_in(seeds[5], 71), 0)
    return dict(coeffs=coeffs, local_coupling=local_coupling, remote_coupling=remote_coupling, beta_coupling=beta_coupling, exc_rows=exc_rows)


def reference(coeffs, local_coupling, remote_coupling, beta_coupling, exc_rows):
    beta_blocks = N // BORD
    beta_wide = beta_coupling.astype(jnp.float32)

    def one_block(block_id):
        own_rows = lax.dynamic_slice_in_dim(coeffs, block_id * ABLK, ABLK, 0)
        sources = exc_rows[block_id].reshape(-1)
        fetched = jnp.take(coeffs, sources, axis=0)
        accumulated = jnp.zeros((ABLK, N), jnp.float32)
        for channel in range(CHANNELS):
            near_mix = jnp.dot(local_coupling[channel, block_id], own_rows, preferred_element_type=jnp.float32).astype(jnp.bfloat16)
            far_coupling = jnp.transpose(remote_coupling[channel, block_id], (1, 0, 2)).reshape(ABLK, SLOTS * ABLK)
            far_mix = jnp.dot(far_coupling, fetched, preferred_element_type=jnp.float32).astype(jnp.bfloat16)
            for mixed in (near_mix, far_mix):
                split_cols = mixed.astype(jnp.float32).reshape(ABLK, beta_blocks, BORD)
                product = jnp.einsum("rkj,kij->rki", split_cols, beta_wide[channel])
                accumulated = accumulated + product.reshape(ABLK, N)
        return accumulated.astype(jnp.bfloat16)

    sigma_half = lax.map(one_block, jnp.arange(N // ABLK, dtype=jnp.int32)).reshape(N, N)
    return (sigma_half.astype(jnp.float32) + sigma_half.T.astype(jnp.float32)).astype(jnp.bfloat16)
```

```python
import jax
import jax.numpy as jnp
from jax import lax
from jax.experimental import pallas as pl
from jax.sharding import PartitionSpec as P

ABLK = 256
AXES = ("alpha", "beta")


def slot_plan(wanted, row_count, owners):
    source_owner = wanted // row_count
    source_row = wanted % row_count
    one_hot = (source_owner[:, None] == jnp.arange(owners, dtype=jnp.int32)[None, :]).astype(
        jnp.int32
    )
    earlier = jnp.cumsum(one_hot, axis=0) - one_hot
    slot_index = jnp.sum(earlier * one_hot, axis=1)
    return (source_owner, source_row, slot_index)


def rows_of(table, index):
    return table.at[index].get(mode="promise_in_bounds")


def mirror_routes(owners, beta_count, turn):
    group = owners // beta_count
    routes = []
    for a in range(owners):
        for b in range(beta_count):
            target = (group * b + (turn + a) % group, a // group)
            routes.append(((a, b), target))
    return routes


def send(value, pairs, beta_count):
    flat = [(s[0] * beta_count + s[1], t[0] * beta_count + t[1]) for s, t in pairs]
    return lax.ppermute(value, AXES, flat)


def mirror_exchange(piece, owners, beta_count, turn, relayed):
    routes = mirror_routes(owners, beta_count, turn)
    if not relayed:
        return send(piece, routes, beta_count)

    def corner(device):
        return (device[0] * 2 // owners, device[1] * 2 // beta_count)

    half_beta = beta_count // 2
    straight = [(s, t) for s, t in routes if corner(s)[0] == corner(s)[1]]
    crossing = [(s, t) for s, t in routes if corner(s)[0] != corner(s)[1]]
    beta_stop = lambda s: (s[0], corner(s)[0] * half_beta + s[1] % half_beta)
    alpha_stop = lambda s, t: (t[0], corner(s)[1] * half_beta + t[1] % half_beta)
    rows = piece.shape[0] // 2
    direct = send(piece, straight, beta_count)
    first = send(piece[:rows], [(s, beta_stop(s)) for s, t in crossing], beta_count)
    second = send(piece[rows:], [(s, alpha_stop(s, t)) for s, t in crossing], beta_count)
    first = send(first, [(beta_stop(s), t) for s, t in crossing], beta_count)
    second = send(second, [(alpha_stop(s, t), t) for s, t in crossing], beta_count)
    me = (lax.axis_index("alpha"), lax.axis_index("beta"))
    is_straight = (me[0] * 2 // owners) == (me[1] * 2 // beta_count)
    return jnp.where(is_straight, direct, jnp.concatenate([first, second], axis=0))


def on_device(coeffs, local_coupling, remote_coupling, beta_coupling, exc_rows):
    row_count, col_count = coeffs.shape
    owners = lax.axis_size("alpha")
    beta_count = lax.axis_size("beta")
    channels, beta_blocks, border, _ = beta_coupling.shape
    blocks = row_count // ABLK
    slot_count = exc_rows.shape[1]
    capacity = 2 * row_count * slot_count // owners
    group = owners // beta_count
    piece_cols = col_count // group
    steps = max(piece_cols // border, 1)
    relayed = owners == 8 and beta_count == 4
    me = lax.axis_index("alpha")

    wanted = exc_rows.reshape(-1)
    source_owner, source_row, slot_index = slot_plan(wanted, row_count, owners)
    flat_slot = source_owner * capacity + slot_index
    request_table = jnp.zeros((owners * capacity,), jnp.int32).at[flat_slot].set(source_row)
    incoming = lax.all_to_all(
        request_table.reshape(owners, capacity), "alpha", split_axis=0, concat_axis=0, tiled=True
    ).reshape(-1)

    far_coupling = jnp.transpose(remote_coupling, (0, 1, 3, 2, 4)).reshape(
        channels, blocks, ABLK, slot_count * ABLK
    )
    alpha_coupling = jnp.concatenate([local_coupling, far_coupling], axis=3)

    def step_blocks(step):
        per_piece = beta_blocks // group
        if per_piece == 0:
            return list(range(beta_blocks))
        return [h * per_piece + step for h in range(group)]

    def columns(array, block):
        return array[:, block * border : (block + 1) * border]

    replies = []
    for step in range(steps):
        own = jnp.concatenate([columns(coeffs, k) for k in step_blocks(step)], axis=1)
        outgoing = rows_of(own, incoming).reshape(owners, capacity, own.shape[1])
        replies.append(
            lax.all_to_all(outgoing, "alpha", split_axis=0, concat_axis=0, tiled=True)
        )

    halves, mirrors = {}, {}
    unit = piece_cols // steps
    ready = flat_slot
    for step in range(steps):
        reply = replies[step].reshape(owners * capacity, -1)
        gathered = rows_of(reply, ready)
        parts = []
        for at, k in enumerate(step_blocks(step)):
            own = columns(coeffs, k).reshape(blocks, ABLK, border)
            far = columns(gathered, at).reshape(blocks, slot_count * ABLK, border)
            both = jnp.concatenate([own, far], axis=1)
            total = None
            for channel in range(channels):
                mix = jnp.einsum(
                    "tij,tjn->tin",
                    alpha_coupling[channel],
                    both,
                    preferred_element_type=jnp.float32,
                ).astype(jnp.bfloat16)
                term = jnp.einsum(
                    "rj,ij->ri",
                    mix.reshape(row_count, border),
                    beta_coupling[channel, k],
                    preferred_element_type=jnp.float32,
                )
                total = term if total is None else total + term
            parts.append(total.astype(jnp.bfloat16))
        if unit != border:
            wide = jnp.concatenate(parts, axis=1)
            parts = [wide[:, h * unit : (h + 1) * unit] for h in range(group)]
        got = []
        for turn in range(group):
            piece = pick(parts, (turn + me) % group)
            got.append(mirror_exchange(piece, owners, beta_count, turn, relayed))
        for h in range(group):
            halves[step, h] = parts[h]
            mirrors[step, h] = pick(got, (me - h) % group)
        if step + 1 < steps:
            held = lax.optimization_barrier(
                (flat_slot, [mirrors[step, h] for h in range(group)])
            )
            ready = held[0]
            for h in range(group):
                mirrors[step, h] = held[1][h]
    return add_mirror(halves, mirrors, row_count, steps, group, unit)


def pick(values, index):
    chosen = values[0]
    for at in range(1, len(values)):
        chosen = jnp.where(index == at, values[at], chosen)
    return chosen


def add_mirror(halves, mirrors, row_count, steps, group, unit):
    tile = min(512, unit)
    per_unit = unit // tile
    down = row_count // tile
    keys = [(step, h) for step in range(steps) for h in range(group)]

    def place(column):
        unit_at = column // per_unit
        return unit_at // steps, unit_at % steps

    def half_map(step, h):
        def index_map(column, row):
            at_h, at_step = place(column)
            mine = jnp.logical_and(at_h == h, at_step == step)
            return jnp.where(mine, row, 0), jnp.where(mine, column % per_unit, 0)

        return index_map

    def mirror_map(step, h):
        def index_map(column, row):
            mine = jnp.logical_and(place(column)[0] == h, row // per_unit == step)
            return jnp.where(mine, column % down, 0), jnp.where(mine, row % per_unit, 0)

        return index_map

    def kernel(*refs):
        half_refs, mirror_refs, out = refs[: len(keys)], refs[len(keys) : -1], refs[-1]
        column, row = pl.program_id(0), pl.program_id(1)
        at_h, at_step = place(column)
        for at, (step, h) in enumerate(keys):
            for row_step in range(steps):
                hit = jnp.logical_and(at_h == h, at_step == step)

                @pl.when(jnp.logical_and(hit, row // per_unit == row_step))
                def _():
                    turned = mirror_refs[keys.index((row_step, h))][...].T
                    total = half_refs[at][...].astype(jnp.float32) + turned.astype(jnp.float32)
                    out[...] = total.astype(out.dtype)

    block = (tile, tile)
    return pl.pallas_call(
        kernel,
        grid=(group * steps * per_unit, down),
        in_specs=[pl.BlockSpec(block, half_map(*key)) for key in keys]
        + [pl.BlockSpec(block, mirror_map(*key)) for key in keys],
        out_specs=pl.BlockSpec(block, lambda column, row: (row, column)),
        out_shape=jax.ShapeDtypeStruct((row_count, group * steps * unit), jnp.bfloat16),
        name="add_mirror",
    )(*[halves[key] for key in keys], *[mirrors[key] for key in keys])


def solution(mesh):
    return jax.shard_map(
        on_device,
        mesh=mesh,
        in_specs=(
            P("alpha", "beta"),
            P(None, "alpha", None, None),
            P(None, "alpha", None, None, None),
            P(None, "beta", None, None),
            P("alpha", None, None),
        ),
        out_specs=P("alpha", "beta"),
        check_vma=False,
    )
```
